512 devices in a mesh: row: 16 (over y_hi, x, core), col: 32 (over y_lo, z).
Axes of the slice: x: 4, y: 4 (y_hi: 2, y_lo: 2; y = y_hi * 2 + y_lo), z: 16, core: 2. Of those that a mesh axis runs over, the one named last changes fastest.
Arguments:
- inputs: bfloat16 [512, 8192], P('col', 'row'), may hold values from -6 to 6
- out_grad: bfloat16 [512, 8192], P('col', 'row'), may hold values from -0.8984375 to 0.8984375
- gate_pre: bfloat16 [512, 16384], P('row', 'col'), may hold values from -6 to 6
- up_pre: bfloat16 [512, 16384], P('row', 'col'), may hold values from -6 to 6
- gate_weight: bfloat16 [8192, 16384], P('row', 'col'), may hold values from -0.0625 to 0.0625
- up_weight: bfloat16 [8192, 16384], P('row', 'col'), may hold values from -0.0625 to 0.0625
- down_weight: bfloat16 [16384, 8192], P('col', 'row'), may hold values from -0.0625 to 0.0625
Outputs:
- input_grad: bfloat16 [512, 8192], P('col', 'row')
- gate_grad: bfloat16 [8192, 16384], P('row', 'col')
- up_grad: bfloat16 [8192, 16384], P('row', 'col')
- down_grad: bfloat16 [16384, 8192], P('col', 'row')
The draws below stay inside these ranges and needn't reach their ends.
All inputs are finite; a program needn't handle non-finite values.
Results may differ from the reference program's by a relative error of at most 0.028.
Values may be sent and summed in bfloat16 or wider, within the bound.
No kernel may reach another device: no remote copies, remote signals or barrier semaphores. Data moves between devices by JAX's collectives and lax.ppermute only.
A program may use at most 64 MiB of HBM per device.

```python
import jax
import jax.numpy as jnp
from jax import lax

D = 8192
FF = 16384
TOKENS = 512
D_BLK = 512
FF_BLK = 512
N_ROW = 16
N_COL = 32


def strengthened(array, own_key, source, target, blocks, factor):
    def block_of(position):
        return (jnp.arange(array.shape[position]) // (array.shape[position] // blocks)).reshape((-1,) + (1,) * (array.ndim - 1 - position))

    first = jax.random.permutation(own_key, blocks)[block_of(target)]
    second = (block_of(target) + blocks // 2) % blocks
    return jnp.where((block_of(source) == first) | (block_of(source) == second), factor * array, array)


def levels(own_key, shape, shards, smallest, top_value):
    loudness = 1.0
    for position, shards_of in shards:
        heights = jax.random.uniform(jax.random.fold_in(jax.random.fold_in(own_key, 6), position), (shards_of,), jnp.float32, smallest / len(shards), top_value / len(shards))
        loudness = loudness * jnp.repeat(jnp.exp(heights), shape[position] // shards_of).reshape((-1,) + (1,) * (len(shape) - 1 - position))
    return loudness


def scatter_about(stream_key, dims, deviation, bound, shards=(), kind=jnp.bfloat16):
    level = levels(stream_key, dims, shards, -0.22, 0.18) if shards else 1.0
    result = jax.random.normal(stream_key, dims, jnp.float32) * deviation * level
    return jnp.minimum(jnp.maximum(result, -bound), bound).astype(kind)


def noise_with(own_key, extent, spread, most, pieces, heavy, kind=jnp.bfloat16):
    result = spread * jax.random.normal(own_key, extent, jnp.float32)
    if pieces:
        result = result * levels(own_key, extent, pieces, -0.22, 0.18)
    return jnp.clip(strengthened(result, jax.random.fold_in(own_key, 3), *heavy), -most, most).astype(kind)


def setup_inputs(seed: int = 0) -> dict:
    splits = jax.random.split(jax.random.key(seed), 8)
    inputs = scatter_about(splits[0], (TOKENS, D), 1.0, 6.0, ((0, 32), (1, 16)))
    out_grad = noise_with(splits[1], (TOKENS, D), 0.15, 0.8984375, ((0, 32), (1, 16)), (1, 0, 32, 2.75))
    gate_pre = scatter_about(splits[2], (TOKENS, FF), 1.0, 6.0, ((0, 16), (1, 32)))
    up_pre = scatter_about(splits[3], (TOKENS, FF), 1.0, 6.0, ((0, 16), (1, 32)))
    gate_weight = scatter_about(splits[4], (D, FF), D ** -0.5, 0.0625, ((0, 16), (1, 32)))
    up_weight = scatter_about(splits[5], (D, FF), D ** -0.5, 0.0625, ((0, 16), (1, 32)))
    down_weight = scatter_about(splits[6], (FF, D), D ** -0.5, 0.0625, ((0, 32), (1, 16)))
    return dict(inputs=inputs, out_grad=out_grad, gate_pre=gate_pre, up_pre=up_pre, gate_weight=gate_weight, up_weight=up_weight, down_weight=down_weight)


def derivatives(gate_pre, up_pre, hidden_grad):
    gate_f32 = gate_pre.astype(jnp.float32)
    up_f32 = up_pre.astype(jnp.float32)
    sigmoid = 1.0 / (1.0 + jnp.exp(-gate_f32))
    activated = gate_f32 * sigmoid
    hidden = (activated * up_f32).astype(jnp.bfloat16)
    gate_delta = (hidden_grad * up_f32 * sigmoid * (1.0 + gate_f32 * (1.0 - sigmoid))).astype(jnp.bfloat16)
    up_delta = (hidden_grad * activated).astype(jnp.bfloat16)
    return hidden, gate_delta, up_delta


def rounded(value):
    narrow = lax.optimization_barrier(value.astype(jnp.bfloat16))
    return narrow.astype(jnp.float32)


def reference(inputs, out_grad, gate_pre, up_pre, gate_weight, up_weight, down_weight):
    by_cols = (((1,), (1,)), ((), ()))
    by_rows = (((0,), (0,)), ((), ()))
    hidden_grad = jnp.zeros((TOKENS, FF), jnp.float32)
    for row_block in range(N_ROW):
        offset = row_block * D_BLK
        block_term = lax.dot_general(out_grad[:, offset:offset + D_BLK], down_weight[:, offset:offset + D_BLK], by_cols, preferred_element_type=jnp.float32)
        hidden_grad = hidden_grad + rounded(block_term)
    hidden, gate_delta, up_delta = derivatives(gate_pre, up_pre, hidden_grad)
    down_grad = lax.dot_general(hidden, out_grad, by_rows, preferred_element_type=jnp.float32).astype(jnp.bfloat16)
    gate_grad = lax.dot_general(inputs, gate_delta, by_rows, preferred_element_type=jnp.float32).astype(jnp.bfloat16)
    up_grad = lax.dot_general(inputs, up_delta, by_rows, preferred_element_type=jnp.float32).astype(jnp.bfloat16)
    input_sum = jnp.zeros((TOKENS, D), jnp.float32)
    for col_block in range(N_COL):
        offset = col_block * FF_BLK
        block_term = lax.dot_general(gate_delta[:, offset:offset + FF_BLK], gate_weight[:, offset:offset + FF_BLK], by_cols, preferred_element_type=jnp.float32)
        block_term = block_term + lax.dot_general(up_delta[:, offset:offset + FF_BLK], up_weight[:, offset:offset + FF_BLK], by_cols, preferred_element_type=jnp.float32)
        input_sum = input_sum + rounded(block_term)
    input_grad = input_sum.astype(jnp.bfloat16)
    return (input_grad, gate_grad, up_grad, down_grad)
```

```python
import jax
import jax.numpy as jnp
from jax import lax
from jax.sharding import Mesh
from jax.sharding import PartitionSpec as P

ROW = ("y_hi", "x_hi", "x_lo", "core")
PLANE = ("y_hi", "x_hi", "x_lo")
COL = ("y_lo", "z3", "z2", "z1", "z_lo")
NEAR = ("y_lo", "z_lo")
FAR = ("z3", "z2", "z1")


def product(x, y, contract):
    return lax.dot_general(
        x, y, (((contract,), (contract,)), ((), ())), preferred_element_type=jnp.float32
    )


def exchanged(blocks, axes):
    return lax.all_to_all(blocks, axes, 0, 0, tiled=True)


def sent_to_all(array, axes):
    peers = lax.axis_size(axes)
    return exchanged(jnp.broadcast_to(array[None], (peers, *array.shape)), axes)


def summed(blocks):
    return blocks.astype(jnp.float32).sum(axis=0)


def grads_gathered(array):
    tokens, width = array.shape
    far = sent_to_all(array, FAR)
    near = sent_to_all(far, NEAR)
    near = near.reshape(lax.axis_size("y_lo"), -1, far.shape[0], tokens, width).swapaxes(1, 2)
    return near.reshape(-1, width)


def doubled(array, axis, place):
    other = lax.ppermute(array, axis, ((0, 1), (1, 0)))
    second = lax.axis_index(axis) == 1
    return jnp.stack((jnp.where(second, other, array), jnp.where(second, array, other)), axis=place)


def inputs_gathered(inputs):
    blocks = doubled(inputs, "z3", 0)
    blocks = doubled(blocks, "z2", 1)
    blocks = doubled(blocks, "z1", 2)
    blocks = doubled(blocks, "z_lo", 3)
    blocks = doubled(blocks, "y_lo", 0)
    return blocks.reshape(-1, inputs.shape[1])


def pre_gathered(gate_pre, up_pre):
    blocks = jnp.stack((gate_pre, up_pre))
    blocks = doubled(blocks, "y_hi", 1)
    blocks = doubled(blocks, "x_hi", 2)
    blocks = doubled(blocks, "x_lo", 3)
    blocks = doubled(blocks, "core", 4)
    return blocks.reshape(2, -1, gate_pre.shape[1])


def hidden_sum(partial):
    peers = lax.axis_size(ROW)
    blocks = partial.reshape(peers, -1, partial.shape[1])
    share = summed(exchanged(blocks, ROW)).astype(jnp.bfloat16)
    plane = sent_to_all(share, PLANE)
    whole = lax.all_gather(plane, "core")
    return whole.swapaxes(0, 1).reshape(-1, share.shape[1])


def input_sum(partial, tokens):
    width = partial.shape[1]
    ys, zs, peers = lax.axis_size("y_lo"), lax.axis_size("z_lo"), lax.axis_size(FAR)
    blocks = partial.reshape(ys, peers, zs, tokens, width).swapaxes(1, 2)
    blocks = blocks.reshape(ys * zs, peers, tokens, width)
    near = summed(exchanged(blocks, NEAR)).astype(jnp.bfloat16)
    return summed(exchanged(near, FAR)).astype(jnp.bfloat16)


def per_device(inputs, out_grad, gate_pre, up_pre, gate_weight, up_weight, down_weight):
    bf16 = jnp.bfloat16
    all_grads = grads_gathered(out_grad)
    gate, up = pre_gathered(gate_pre, up_pre).astype(jnp.float32)
    all_inputs = inputs_gathered(inputs)
    hidden_grad = hidden_sum(product(all_grads, down_weight, 1).astype(bf16)).astype(jnp.float32)
    sigmoid = 1.0 / (1.0 + jnp.exp(-gate))
    silu = gate * sigmoid
    hidden = (silu * up).astype(bf16)
    gate_delta = (hidden_grad * up * sigmoid * (1.0 + gate * (1.0 - sigmoid))).astype(bf16)
    up_delta = (hidden_grad * silu).astype(bf16)
    partial = product(gate_delta, gate_weight, 1) + product(up_delta, up_weight, 1)
    input_grad = input_sum(partial.astype(bf16), inputs.shape[0])
    down_grad = product(hidden, all_grads, 0).astype(bf16)
    gate_grad = product(all_inputs, gate_delta, 0).astype(bf16)
    up_grad = product(all_inputs, up_delta, 0).astype(bf16)
    return input_grad, gate_grad, up_grad, down_grad


def solution(mesh):
    split = Mesh(mesh.devices.reshape(2, 2, 2, 2, 2, 2, 2, 2, 2), ROW + COL)
    tokens_by_col, tokens_by_row = P(COL, ROW), P(ROW, COL)
    in_specs = (
        tokens_by_col,
        tokens_by_col,
        tokens_by_row,
        tokens_by_row,
        tokens_by_row,
        tokens_by_row,
        tokens_by_col,
    )
    out_specs = (tokens_by_col, tokens_by_row, tokens_by_row, tokens_by_col)
    return jax.shard_map(
        per_device, mesh=split, in_specs=in_specs, out_specs=out_specs, check_vma=False
    )
```

```python
import jax
import jax.numpy as jnp
from jax import lax
from jax.sharding import Mesh
from jax.sharding import PartitionSpec as P

GRID = ("y_hi", "x_hi", "x_lo", "core")
ROW = ("core", "y_hi", "x_hi", "x_lo")
PLANE = ("y_hi", "x_hi", "x_lo")
COL = ("y_lo", "z3", "z2", "z1", "z_lo")
NEAR = ("y_lo", "z_lo")
FAR = ("z3", "z2", "z1")


def product(x, y, contract):
    return lax.dot_general(
        x, y, (((contract,), (contract,)), ((), ())), preferred_element_type=jnp.float32
    )


def exchanged(blocks, axes):
    return lax.all_to_all(blocks, axes, 0, 0, tiled=True)


def sent_to_all(array, axes):
    peers = lax.axis_size(axes)
    return exchanged(jnp.broadcast_to(array[None], (peers, *array.shape)), axes)


def summed(blocks):
    return blocks.astype(jnp.float32).sum(axis=0)


def far_gathered(out_grad, inputs):
    first = lax.broadcasted_iota(jnp.int32, (lax.axis_size(FAR), 2, 1, 1), 1) == 0
    far = exchanged(jnp.where(first, out_grad, inputs), FAR)
    return far[:, 0], far[:, 1]


def grads_gathered(far):
    return sent_to_all(far, NEAR).reshape(-1, far.shape[2])


def doubled(array, axis, place):
    other = lax.ppermute(array, axis, ((0, 1), (1, 0)))
    second = lax.axis_index(axis) == 1
    return jnp.stack((jnp.where(second, other, array), jnp.where(second, array, other)), axis=place)


def inputs_gathered(far):
    blocks = doubled(far, "z_lo", 0)
    blocks = doubled(blocks, "y_lo", 0)
    return blocks.reshape(-1, far.shape[2])


def pre_gathered(gate_pre, up_pre):
    _, width = gate_pre.shape
    blocks = jnp.stack((gate_pre, up_pre)).reshape(2, lax.axis_size("z_lo"), -1, width)
    blocks = doubled(blocks, "y_hi", 1)
    blocks = doubled(blocks, "x_hi", 3)
    blocks = doubled(blocks, "x_lo", 4)
    blocks = doubled(blocks, "core", 5)
    return lax.optimization_barrier((blocks[0].reshape(-1, width), blocks[1].reshape(-1, width)))


def hidden_sum(partial):
    width = partial.shape[1]
    blocks = partial.reshape(lax.axis_size(ROW), -1, width)
    share = summed(exchanged(blocks, ROW)).astype(jnp.bfloat16)
    plane = sent_to_all(share, PLANE)
    return lax.all_gather(plane, "core").reshape(-1, width)


def near_sum(partial, tokens):
    blocks = partial.reshape(lax.axis_size(NEAR), -1, tokens, partial.shape[1])
    return summed(exchanged(blocks, NEAR)).astype(jnp.bfloat16)


def far_sum(blocks):
    return summed(exchanged(blocks, FAR)).astype(jnp.bfloat16)


def hidden_of(pre):
    gate, up = pre[0].astype(jnp.float32), pre[1].astype(jnp.float32)
    return (gate / (1.0 + jnp.exp(-gate)) * up).astype(jnp.bfloat16)


def deltas(pre, hidden_grad):
    gate, up = pre[0].astype(jnp.float32), pre[1].astype(jnp.float32)
    grad = hidden_grad.astype(jnp.float32)
    sigmoid = 1.0 / (1.0 + jnp.exp(-gate))
    gate_delta = grad * up * sigmoid * (1.0 + gate * (1.0 - sigmoid))
    return gate_delta.astype(jnp.bfloat16), (grad * (gate * sigmoid)).astype(jnp.bfloat16)


def per_device(inputs, out_grad, gate_pre, up_pre, gate_weight, up_weight, down_weight):
    bf16 = jnp.bfloat16
    far_grads, far_inputs = far_gathered(out_grad, inputs)
    all_grads = grads_gathered(far_grads)
    all_inputs = inputs_gathered(far_inputs)
    pre = pre_gathered(gate_pre, up_pre)
    hidden, *pre = lax.optimization_barrier((hidden_of(pre), *pre))
    hidden_grad = hidden_sum(product(all_grads, down_weight, 1).astype(bf16))
    gate_delta, up_delta = lax.optimization_barrier(deltas(pre, hidden_grad))
    partial = product(gate_delta, gate_weight, 1) + product(up_delta, up_weight, 1)
    near = near_sum(partial.astype(bf16), inputs.shape[0])
    input_grad = far_sum(near)
    down_grad = product(hidden, all_grads, 0).astype(bf16)
    gate_grad = product(all_inputs, gate_delta, 0).astype(bf16)
    up_grad = product(all_inputs, up_delta, 0).astype(bf16)
    return input_grad, gate_grad, up_grad, down_grad


def solution(mesh):
    split = Mesh(mesh.devices.reshape(2, 2, 2, 2, 2, 2, 2, 2, 2), GRID + COL)
    tokens_by_col, tokens_by_row = P(COL, GRID), P(GRID, COL)
    in_specs = (
        tokens_by_col,
        tokens_by_col,
        tokens_by_row,
        tokens_by_row,
        tokens_by_row,
        tokens_by_row,
        tokens_by_col,
    )
    out_specs = (tokens_by_col, tokens_by_row, tokens_by_row, tokens_by_col)
    return jax.shard_map(
        per_device, mesh=split, in_specs=in_specs, out_specs=out_specs, check_vma=False
    )
```

```python
import jax
import jax.numpy as jnp
from jax import lax
from jax.sharding import Mesh
from jax.sharding import PartitionSpec as P

GRID = ("y_hi", "x_hi", "x_lo", "core")
ROW = ("core", "y_hi", "x_hi", "x_lo")
PLANE = ("y_hi", "x_hi", "x_lo")
COL = ("y_lo", "z3", "z2", "z1", "z_lo")
NEAR = ("y_lo", "z_lo")
FAR = ("z3", "z2", "z1")


def product(x, y, contract):
    return lax.dot_general(
        x, y, (((contract,), (contract,)), ((), ())), preferred_element_type=jnp.float32
    )


def exchanged(blocks, axes):
    return lax.all_to_all(blocks, axes, 0, 0, tiled=True)


def sent_to_all(array, axes):
    peers = lax.axis_size(axes)
    return exchanged(jnp.broadcast_to(array[None], (peers, *array.shape)), axes)


def summed(blocks):
    return blocks.astype(jnp.float32).sum(axis=0)


def far_gathered(out_grad, inputs):
    first = lax.broadcasted_iota(jnp.int32, (lax.axis_size(FAR), 2, 1, 1), 1) == 0
    far = exchanged(jnp.where(first, out_grad, inputs), FAR)
    return far[:, 0], far[:, 1]


def grads_gathered(far):
    return sent_to_all(far, NEAR).reshape(-1, far.shape[2])


def doubled(array, axis, place):
    other = lax.ppermute(array, axis, ((0, 1), (1, 0)))
    second = lax.axis_index(axis) == 1
    return jnp.stack(
        (jnp.where(second, other, array), jnp.where(second, array, other)), axis=place
    )


def inputs_gathered(far):
    blocks = doubled(far, "z_lo", 0)
    blocks = doubled(blocks, "y_lo", 0)
    return blocks.reshape(-1, far.shape[2])


def pre_gathered(gate_pre, up_pre):
    _, width = gate_pre.shape
    blocks = jnp.stack((gate_pre, up_pre)).reshape(2, lax.axis_size("z_lo"), -1, width)
    blocks = doubled(blocks, "y_hi", 1)
    blocks = doubled(blocks, "x_hi", 3)
    blocks = doubled(blocks, "x_lo", 4)
    blocks = doubled(blocks, "core", 5)
    return blocks[0].reshape(-1, width), blocks[1].reshape(-1, width)


def hidden_sum(partial):
    width = partial.shape[1]
    blocks = partial.reshape(lax.axis_size(ROW), -1, width)
    share = summed(exchanged(blocks, ROW)).astype(jnp.bfloat16)
    plane = sent_to_all(share, PLANE)
    return lax.all_gather(plane, "core").reshape(-1, width)


def near_sum(partial, tokens):
    blocks = partial.reshape(lax.axis_size(NEAR), -1, tokens, partial.shape[1])
    return summed(exchanged(blocks, NEAR)).astype(jnp.bfloat16)


def far_sum(blocks):
    return summed(exchanged(blocks, FAR)).astype(jnp.bfloat16)


def hidden_of(pre):
    gate, up = pre[0].astype(jnp.float32), pre[1].astype(jnp.float32)
    return (gate / (1.0 + jnp.exp(-gate)) * up).astype(jnp.bfloat16)


def deltas(pre, hidden_grad):
    gate, up = pre[0].astype(jnp.float32), pre[1].astype(jnp.float32)
    grad = hidden_grad.astype(jnp.float32)
    sigmoid = 1.0 / (1.0 + jnp.exp(-gate))
    gate_delta = grad * up * sigmoid * (1.0 + gate * (1.0 - sigmoid))
    return gate_delta.astype(jnp.bfloat16), (grad * (gate * sigmoid)).astype(jnp.bfloat16)


def per_device(inputs, out_grad, gate_pre, up_pre, gate_weight, up_weight, down_weight):
    bf16 = jnp.bfloat16
    far_grads, far_inputs = far_gathered(out_grad, inputs)
    all_grads = grads_gathered(far_grads)
    all_inputs = inputs_gathered(far_inputs)
    pre = pre_gathered(gate_pre, up_pre)
    hidden, *pre = lax.optimization_barrier((hidden_of(pre), *pre))
    hidden_grad = hidden_sum(product(all_grads, down_weight, 1).astype(bf16))
    gate_delta, up_delta = lax.optimization_barrier(deltas(pre, hidden_grad))
    partial = product(gate_delta, gate_weight, 1) + product(up_delta, up_weight, 1)
    near = near_sum(partial.astype(bf16), inputs.shape[0])
    input_grad = far_sum(near)
    down_grad = product(hidden, all_grads, 0).astype(bf16)
    gate_grad = product(all_inputs, gate_delta, 0).astype(bf16)
    up_grad = product(all_inputs, up_delta, 0).astype(bf16)
    return input_grad, gate_grad, up_grad, down_grad


def solution(mesh):
    split = Mesh(mesh.devices.reshape(2, 2, 2, 2, 2, 2, 2, 2, 2), GRID + COL)
    tokens_by_col, tokens_by_row = P(COL, GRID), P(GRID, COL)
    in_specs = (
        tokens_by_col,
        tokens_by_col,
        tokens_by_row,
        tokens_by_row,
        tokens_by_row,
        tokens_by_row,
        tokens_by_col,
    )
    out_specs = (tokens_by_col, tokens_by_row, tokens_by_row, tokens_by_col)
    return jax.shard_map(
        per_device, mesh=split, in_specs=in_specs, out_specs=out_specs, check_vma=False
    )
```
